32 devices in a mesh: strings: 2 (over y), ka: 4 (over x, core), coef: 4 (over z).
Axes of the slice: x: 2, y: 2, z: 4, core: 2. Of those that a mesh axis runs over, the one named last changes fastest.
Arguments:
- wavefunctions: float32 [8, 49152, 384], P(('strings', 'ka'), 'coef'), parts along dimension 0, may hold values from -8 to 8
Outputs:
- transported: float32 [8, 49152, 384], P(('strings', 'ka'), 'coef'), parts along dimension 0
The draws below stay inside these ranges and needn't reach their ends.
There are 2 independent parts, one for each index of `strings`. The reference program is written for one: setup_inputs(seed, part) draws one part's arguments, and reference() takes and returns one part's arrays. A program takes and returns all parts, laid end to end along the dimension named above; each array names one. Nothing has to cross between parts.
All inputs are finite; a program needn't handle non-finite values.
Results may differ from the reference program's by a relative error of at most 0.0003.
Values sent between devices are 32-bit elements; how exact they have to be, the bound alone decides.
No kernel may reach another device: no remote copies, remote signals or barrier semaphores. Data moves between devices by JAX's collectives and lax.ppermute only.
A program may use at most 128 MiB of HBM per device.

```python
import jax
import jax.numpy as jnp
from jax import lax

G = 49152
NB = 384
NS_ITERS = 3
K = 4


def draw_wavefunctions(key, part):
    key_base, key_frames = jax.random.split(jax.random.fold_in(key, 11), 2)
    base = jax.random.normal(key_base, (G, NB), jnp.float32)
    identity = jnp.eye(NB, dtype=jnp.float32)

    def one_point(index_k):
        subkey = jax.random.fold_in(key_frames, index_k)
        key_skew, key_mix, key_noise = jax.random.split(subkey, 3)
        skew_raw = jax.random.normal(key_skew, (NB, NB), jnp.float32) * (0.6 / jnp.sqrt(NB * 1.0))
        skew = skew_raw - skew_raw.T
        rotation = jnp.linalg.solve(identity - skew, identity + skew)
        mixing = identity + 0.1 * jax.random.normal(key_mix, (NB, NB), jnp.float32) / jnp.sqrt(NB * 1.0)
        frame = jnp.dot(rotation, mixing, precision=lax.Precision.HIGHEST)
        noise = 0.3 * jax.random.normal(key_noise, (G, NB), jnp.float32)
        values = jnp.dot(base, frame, precision=lax.Precision.HIGHEST) + noise
        return jnp.clip(values, -8.0, 8.0)
    return lax.map(one_point, jnp.arange(K, dtype=jnp.int32))


def setup_inputs(seed: int = 0, part: int = 0) -> dict:
    key_of = jax.random.split(jax.random.key(seed), 2)
    part_keys = jax.random.split(jax.random.fold_in(key_of[1], part), 2)
    wavefunctions = draw_wavefunctions(jax.random.fold_in(jax.random.fold_in(key_of[1], part), 71), part)
    return dict(wavefunctions=wavefunctions)


def polar_factor(matrix):
    norm_scale = jnp.sqrt(NB * jnp.mean(matrix * matrix) + 1e-06)
    iterate = matrix / norm_scale
    for iteration in range(NS_ITERS):
        gram_matrix = jnp.dot(iterate.T, iterate, precision=lax.Precision.HIGHEST)
        iterate = 1.5 * iterate - 0.5 * jnp.dot(iterate, gram_matrix, precision=lax.Precision.HIGHEST)
    return iterate

def reference(wavefunctions):
    indices = jnp.arange(K, dtype=jnp.int32)

    def unitary_at(index_k):
        before_k = jnp.where(index_k == 0, K - 1, index_k - 1).astype(jnp.int32)
        earlier = lax.dynamic_index_in_dim(wavefunctions, before_k, 0, keepdims=False)
        current = lax.dynamic_index_in_dim(wavefunctions, index_k, 0, keepdims=False)
        margin = jnp.dot(earlier.T, current, precision=lax.Precision.HIGHEST) / G
        return polar_factor(margin)
    unitaries = lax.map(unitary_at, indices)

    def advance(product, unitary):
        product = jnp.dot(product, unitary, precision=lax.Precision.HIGHEST)
        return (product, product)
    start = jnp.eye(NB, dtype=jnp.float32)
    last_product, products = lax.scan(advance, start, unitaries)

    def rotate(index_k):
        current = lax.dynamic_index_in_dim(wavefunctions, index_k, 0, keepdims=False)
        product = lax.dynamic_index_in_dim(products, index_k, 0, keepdims=False)
        return jnp.dot(current, product.T, precision=lax.Precision.HIGHEST)
    return lax.map(rotate, indices)
```

```python
import functools

import jax
import jax.numpy as jnp
from jax import lax
from jax.experimental import pallas as pl
from jax.experimental.pallas import tpu as pltpu
from jax.sharding import PartitionSpec as P


NS_ITERS = 3
F32 = jnp.float32
BF16 = jnp.bfloat16


def split(x):
    high = x.astype(BF16)
    return high, (x - high.astype(F32)).astype(BF16)


def dot(a, b):
    return lax.dot_general(a, b, (((1,), (0,)), ((), ())), preferred_element_type=F32)


def product3(a, b):
    size = b[0].shape[1]
    wide = dot(a[0], jnp.concatenate(b, axis=1))
    return wide[:, :size] + (wide[:, size:] + dot(a[1], b[0]))


def polar(matrix, total):
    size = matrix.shape[0]
    margin = matrix * (1.0 / total)
    scale = jnp.sqrt(size * (jnp.sum(margin * margin) / (size * size)) + 1e-06)
    iterate = margin / scale
    for _ in range(NS_ITERS):
        parts = split(iterate)
        gram = product3(split(iterate.T), parts)
        iterate = 1.5 * iterate - 0.5 * product3(parts, split(gram))
    return iterate


def polar_kernel(total, sum_ref, out_ref):
    out_ref[...] = polar(sum_ref[...], total)


VMEM = pl.BlockSpec(memory_space=pltpu.VMEM)


def polar_call(matrix, total):
    return pl.pallas_call(
        functools.partial(polar_kernel, total),
        out_shape=jax.ShapeDtypeStruct(matrix.shape, F32),
        in_specs=[VMEM],
        out_specs=VMEM,
        name="polar",
    )(matrix)


def rotate_kernel(total, rows_ref, turned_ref, later_ref, wave, out, wave_buf, out_buf, near_ref, rest_ref, low_ref, in_sem, out_sem):
    size = wave_buf.shape[1]
    block = out_buf.shape[1]
    steps = wave_buf.shape[0] // block
    main = size // 256 * 256
    rest = size - main

    def fetch(c):
        piece = pl.ds(pl.multiple_of(c * block, block), block)
        return pltpu.make_async_copy(wave.at[piece], wave_buf.at[piece], in_sem.at[c])

    def put(c):
        piece = pl.ds(pl.multiple_of(c * block, block), block)
        return pltpu.make_async_copy(out_buf.at[c % 2], out.at[piece], out_sem.at[c % 2])

    for c in range(steps):
        fetch(c).start()
    closing = polar(rows_ref[...] + turned_ref[...].T, total)
    high, low = split(product3(split(later_ref[...].T), split(closing.T)))
    near_ref[0:size] = high[:, :main]
    near_ref[size:] = high[:, :main]
    rest_ref[0:size, :rest] = high[:, main:]
    rest_ref[size:, :rest] = high[:, main:]
    rest_ref[0:size, rest:] = low[:, main:]
    rest_ref[size:, rest:] = jnp.zeros((size, rest), BF16)
    low_ref[...] = low[:, :main]

    def body(c, _):
        fetch(c).wait()

        @pl.when(c >= 2)
        def _():
            put(c - 2).wait()

        high, low = split(wave_buf[pl.ds(pl.multiple_of(c * block, block), block)])
        both = jnp.concatenate([high, low], axis=1)
        out_buf[c % 2, :, :main] = dot(both, near_ref[...]) + dot(high, low_ref[...])
        wide = dot(both, rest_ref[...])
        out_buf[c % 2, :, main:] = wide[:, :rest] + wide[:, rest:]
        put(c).start()
        return 0

    lax.fori_loop(0, steps, body, 0)
    for c in range(max(steps - 2, 0), steps):
        put(c).wait()


def rotate_call(rows, turned, later, wave, total):
    count, size = wave.shape
    block = 1024
    while count % block:
        block //= 2
    main = size // 256 * 256
    rest = size - main
    hbm = pl.BlockSpec(memory_space=pltpu.HBM)
    return pl.pallas_call(
        functools.partial(rotate_kernel, total),
        out_shape=jax.ShapeDtypeStruct(wave.shape, F32),
        in_specs=[VMEM, VMEM, VMEM, hbm],
        out_specs=hbm,
        scratch_shapes=[
            pltpu.VMEM((count, size), F32),
            pltpu.VMEM((2, block, size), F32),
            pltpu.VMEM((2 * size, main), BF16),
            pltpu.VMEM((2 * size, 2 * rest), BF16),
            pltpu.VMEM((size, main), BF16),
            pltpu.SemaphoreType.DMA((count // block,)),
            pltpu.SemaphoreType.DMA((2,)),
        ],
        name="rotate",
    )(rows, turned, later, wave)


def xdot(a, b):
    return lax.dot_general(a, b, (((0,), (0,)), ((), ())), precision=lax.Precision.HIGH)


def few(axis):
    return lax.axis_size(axis) in (2, 4)


def xor_permute(x, distance, ends_only=False):
    points, count = lax.axis_size("ka"), lax.axis_size("coef")
    some = (0, points - 1) if ends_only else range(points)
    route = [(k * count + i, k * count + (i ^ distance)) for k in some for i in range(count)]
    return lax.ppermute(x, ("ka", "coef"), route)


def scatter_sum(x, ends_only=False):
    count = lax.axis_size("coef")
    if not few("coef"):
        return lax.psum_scatter(x, "coef", scatter_dimension=0, tiled=True)
    share = x.shape[0] // count
    me = lax.axis_index("coef")
    total = lax.dynamic_slice_in_dim(x, me * share, share, 0)
    parts = [
        xor_permute(lax.dynamic_slice_in_dim(x, (me ^ d) * share, share, 0), d, ends_only)
        for d in range(count - 1, 0, -1)
    ]
    for part in parts:
        total = total + part
    return total


def gather_rows(x, ends_only=False):
    count = lax.axis_size("coef")
    if not few("coef"):
        return lax.all_gather(x, "coef", axis=0, tiled=True)
    me = lax.axis_index("coef")
    pieces = jnp.stack([x] + [xor_permute(x, d, ends_only) for d in range(1, count)])
    return jnp.concatenate(
        [lax.dynamic_index_in_dim(pieces, me ^ j, 0, keepdims=False) for j in range(count)]
    )


def end_sum(x):
    count = lax.axis_size("coef")
    if not few("coef"):
        return lax.psum(x, "coef")
    total = x
    for d in range(count - 1, 0, -1):
        total = total + xor_permute(x, d, True)
    return total


def ends(x):
    count = lax.axis_size("ka")
    if count != 4:
        both = lax.all_gather(x, "ka", axis=0)
        return both[0], both[count - 1]
    me = lax.axis_index("ka")
    across = lax.ppermute(x, "ka", [(0, 2), (3, 1)])
    own = jnp.where((me == 0) | (me == 3), x, across)
    other = lax.ppermute(own, "ka", [(0, 1), (1, 0), (2, 3), (3, 2)])
    even = (me == 0) | (me == 2)
    return jnp.where(even, own, other), jnp.where(even, other, own)


def after(x, *others):
    return lax.optimization_barrier((x,) + others)[0]


HBM = pl.BlockSpec(memory_space=pltpu.HBM)


def copy_rows_kernel(pieces, wave, *refs):
    outs = refs[: len(pieces)]
    bufs = refs[len(pieces) : 2 * len(pieces)]
    in_sem, out_sem = refs[2 * len(pieces) :]
    ins = [
        pltpu.make_async_copy(wave.at[pl.ds(low, high - low)], buf, in_sem.at[i])
        for i, ((low, high), buf) in enumerate(zip(pieces, bufs))
    ]
    puts = [pltpu.make_async_copy(buf, out, out_sem.at[i]) for i, (buf, out) in enumerate(zip(bufs, outs))]
    for copy in ins:
        copy.start()
    for get, put in zip(ins, puts):
        get.wait()
        put.start()
    for put in puts:
        put.wait()


def copy_rows(wave, pieces):
    size = wave.shape[1]
    shapes = [(high - low, size) for low, high in pieces]
    return pl.pallas_call(
        functools.partial(copy_rows_kernel, pieces),
        out_shape=[jax.ShapeDtypeStruct(s, F32) for s in shapes],
        in_specs=[HBM],
        out_specs=[HBM] * len(pieces),
        scratch_shapes=[pltpu.VMEM(s, F32) for s in shapes]
        + [pltpu.SemaphoreType.DMA((len(pieces),)), pltpu.SemaphoreType.DMA((len(pieces),))],
        name="copy_rows",
    )(wave)


def cuts(unit, shares):
    bounds = [0]
    for share in shares:
        bounds.append(bounds[-1] + share * unit)
    return list(zip(bounds[:-1], bounds[1:]))


def cut_kernel(pieces, start, wave, *refs):
    outs = refs[: len(pieces)]
    buf, in_sem, out_sem = refs[len(pieces) :]
    half, _ = buf.shape
    begin = pl.multiple_of(start[0], 8)
    share = half // in_sem.shape[0]
    gets = [
        pltpu.make_async_copy(
            wave.at[pl.ds(begin + i * share, share)], buf.at[pl.ds(i * share, share)], in_sem.at[i]
        )
        for i in range(in_sem.shape[0])
    ]
    puts = [
        pltpu.make_async_copy(
            buf.at[pl.ds(low, high - low), pl.ds(left, right - left)], out, out_sem.at[i]
        )
        for i, (((low, high), (left, right)), out) in enumerate(zip(pieces, outs))
    ]
    for get in gets:
        get.start()
    landed = 0
    for ((low, high), _), put in zip(pieces, puts):
        while landed * share < high:
            gets[landed].wait()
            landed += 1
        put.start()
    for get in gets[landed:]:
        get.wait()
    for put in puts:
        put.wait()


def cut_call(wave, start, half, pieces):
    shapes = [(high - low, right - left) for (low, high), (left, right) in pieces]
    return pl.pallas_call(
        functools.partial(cut_kernel, pieces),
        out_shape=[jax.ShapeDtypeStruct(s, F32) for s in shapes],
        in_specs=[pl.BlockSpec(memory_space=pltpu.SMEM), HBM],
        out_specs=[HBM] * len(shapes),
        scratch_shapes=[
            pltpu.VMEM((half, wave.shape[1]), F32),
            pltpu.SemaphoreType.DMA((6,)),
            pltpu.SemaphoreType.DMA((len(shapes),)),
        ],
        name="cut",
    )(jnp.reshape(start, (1,)).astype(jnp.int32), wave)


FIRSTS = (2, 5, 4, 1)
WIDES = (6, 6)
LATES = (4, 4, 3, 1)


def whole_step(wavefunctions):
    wave = wavefunctions[0]
    count, size = wave.shape
    points = lax.axis_size("ka")
    position = lax.axis_index("ka")
    coefs = lax.axis_size("coef")
    total = count * coefs
    half = count // 2
    unit = half // 12
    wide = size - 128
    forward = [(k, k + 1) for k in range(points - 1)]
    backward = [(k + 1, k) for k in range(points - 1)]
    closing = [(0, points - 1), (points - 1, 0)]
    streamed = []

    def stream(pieces, behind):
        tie = streamed[behind] if behind is not None else ()
        streamed.append(tuple(lax.ppermute(after(x, *tie), "ka", way) for x, way in pieces))

    firsts = cuts(unit, FIRSTS)
    for i, (low, high) in enumerate(firsts):
        up, down = copy_rows(wave, [(low, high), (half + low, half + high)])
        stream(((up, forward), (down, backward)), i - 2 if i >= 2 else None)

    start = jnp.where(position == 0, 0, half)
    local_at = half - start
    wides, lates = cuts(unit, WIDES), cuts(unit, LATES)
    blocks = [(rows, (0, wide)) for rows in wides] + [(rows, (wide, size)) for rows in lates]
    for block in cut_call(wave, start, half, blocks):
        i = len(streamed)
        stream(((block, closing),), i - 2 if i < len(firsts) + len(wides) else i - 3)

    def local(rows):
        return lax.dynamic_slice_in_dim(wave, local_at + rows[0], rows[1] - rows[0], 0)

    at_later = at_earlier = jnp.zeros((size, size), F32)
    for i, (low, high) in enumerate(firsts):
        up, down = streamed[i]
        at_later = at_later + xdot(up, wave[low:high])
        at_earlier = at_earlier + xdot(wave[half + low : half + high], down)

    both = jnp.stack([at_later, at_earlier])
    share = size // coefs
    both = scatter_sum(both.reshape(2, coefs, share, size).transpose(1, 0, 2, 3).reshape(2 * size, size))
    margin_share = both[:share] + lax.ppermute(both[share:], "ka", forward)
    unitary = polar_call(gather_rows(margin_share), total)

    early = jnp.zeros((wide, size), F32)
    at = len(firsts)
    early = early + xdot(after(streamed[at][0], unitary), local(wides[0]))

    mine = lax.axis_index("coef")
    own = jnp.where(position == 0, jnp.eye(size, dtype=F32), after(unitary, early))
    product = lax.dynamic_slice_in_dim(own, mine * share, share, 0)
    for k in range(1, points - 1):
        came = lax.ppermute(product, "ka", [(k, k + 1)])
        longer = lax.dot_general(came, own, (((1,), (0,)), ((), ())), precision=lax.Precision.HIGH)
        product = jnp.where(position == k + 1, longer, product)
    later = gather_rows(product)

    early = early + xdot(after(streamed[at + 1][0], later), local(wides[1]))

    early = ends(gather_rows(scatter_sum(early, True), True))
    late = jnp.zeros((128, size), F32)
    for i, rows in enumerate(lates):
        late = late + xdot(streamed[at + 2 + i][0], local(rows))
    late = ends(end_sum(late))
    rows, turned = [jnp.concatenate(pair) for pair in zip(early, late)]
    return rotate_call(rows, turned, later, wave, total)[None]


def solution(mesh):
    spec = P(("strings", "ka"), "coef", None)
    return jax.shard_map(whole_step, mesh=mesh, in_specs=(spec,), out_specs=spec, check_vma=False)
```

```python
import functools
import math

import jax
import jax.numpy as jnp
from jax import lax
from jax.experimental import pallas as pl
from jax.experimental.pallas import tpu as pltpu
from jax.sharding import PartitionSpec as P


NS_ITERS = 3
F32 = jnp.float32
BF16 = jnp.bfloat16


def split(x):
    high = x.astype(BF16)
    return high, (x - high.astype(F32)).astype(BF16)


def dot(a, b):
    return lax.dot_general(a, b, (((1,), (0,)), ((), ())), preferred_element_type=F32)


def product3(a, b):
    size = b[0].shape[1]
    wide = dot(a[0], jnp.concatenate(b, axis=1))
    return wide[:, :size] + (wide[:, size:] + dot(a[1], b[0]))


def polar(matrix, total):
    size = matrix.shape[0]
    margin = matrix * (1.0 / total)
    scale = jnp.sqrt(size * (jnp.sum(margin * margin) / (size * size)) + 1e-06)
    iterate = margin / scale
    for _ in range(NS_ITERS):
        parts = split(iterate)
        gram = product3(split(iterate.T), parts)
        iterate = 1.5 * iterate - 0.5 * product3(parts, split(gram))
    return iterate


def polar_kernel(total, sum_ref, *refs):
    refs[-1][...] = polar(sum_ref[...], total)


VMEM = pl.BlockSpec(memory_space=pltpu.VMEM)
HBM = pl.BlockSpec(memory_space=pltpu.HBM)
ANY = pl.BlockSpec(memory_space=pl.ANY)


def polar_call(matrix, total, behind):
    return pl.pallas_call(
        functools.partial(polar_kernel, total),
        out_shape=jax.ShapeDtypeStruct(matrix.shape, F32),
        in_specs=[VMEM, ANY],
        out_specs=VMEM,
        name="polar",
    )(matrix, behind)


def rotate_kernel(total, rows_ref, turned_ref, later_ref, wave, out, wave_buf, out_buf, near_ref, rest_ref, low_ref, in_sem, out_sem):
    size = wave_buf.shape[1]
    block = out_buf.shape[1]
    steps = wave_buf.shape[0] // block
    main = size // 256 * 256
    rest = size - main

    def fetch(c):
        piece = pl.ds(pl.multiple_of(c * block, block), block)
        return pltpu.make_async_copy(wave.at[piece], wave_buf.at[piece], in_sem.at[c])

    def put(c):
        piece = pl.ds(pl.multiple_of(c * block, block), block)
        return pltpu.make_async_copy(out_buf.at[c % 2], out.at[piece], out_sem.at[c % 2])

    for c in range(steps):
        fetch(c).start()
    closing = polar(rows_ref[...] + turned_ref[...].T, total)
    high, low = split(product3(split(later_ref[...].T), split(closing.T)))
    near_ref[0:size] = high[:, :main]
    near_ref[size:] = high[:, :main]
    rest_ref[0:size, :rest] = high[:, main:]
    rest_ref[size:, :rest] = high[:, main:]
    rest_ref[0:size, rest:] = low[:, main:]
    rest_ref[size:, rest:] = jnp.zeros((size, rest), BF16)
    low_ref[...] = low[:, :main]

    def body(c, _):
        fetch(c).wait()

        @pl.when(c >= 2)
        def _():
            put(c - 2).wait()

        high, low = split(wave_buf[pl.ds(pl.multiple_of(c * block, block), block)])
        both = jnp.concatenate([high, low], axis=1)
        out_buf[c % 2, :, :main] = dot(both, near_ref[...]) + dot(high, low_ref[...])
        wide = dot(both, rest_ref[...])
        out_buf[c % 2, :, main:] = wide[:, :rest] + wide[:, rest:]
        put(c).start()
        return 0

    lax.fori_loop(0, steps, body, 0)
    for c in range(max(steps - 2, 0), steps):
        put(c).wait()


def rotate_call(rows, turned, later, wave, total):
    count, size = wave.shape
    block = 1024
    while count % block:
        block //= 2
    main = size // 256 * 256
    rest = size - main
    hbm = pl.BlockSpec(memory_space=pltpu.HBM)
    return pl.pallas_call(
        functools.partial(rotate_kernel, total),
        out_shape=jax.ShapeDtypeStruct(wave.shape, F32),
        in_specs=[VMEM, VMEM, VMEM, hbm],
        out_specs=hbm,
        scratch_shapes=[
            pltpu.VMEM((count, size), F32),
            pltpu.VMEM((2, block, size), F32),
            pltpu.VMEM((2 * size, main), BF16),
            pltpu.VMEM((2 * size, 2 * rest), BF16),
            pltpu.VMEM((size, main), BF16),
            pltpu.SemaphoreType.DMA((count // block,)),
            pltpu.SemaphoreType.DMA((2,)),
        ],
        name="rotate",
    )(rows, turned, later, wave)


def few(axis):
    return lax.axis_size(axis) in (2, 4)


def xor_permute(x, distance, ends_only=False):
    points, count = lax.axis_size("ka"), lax.axis_size("coef")
    some = (0, points - 1) if ends_only else range(points)
    route = [(k * count + i, k * count + (i ^ distance)) for k in some for i in range(count)]
    return lax.ppermute(x, ("ka", "coef"), route)


def scatter_sum(x, ends_only=False):
    count = lax.axis_size("coef")
    if not few("coef"):
        return lax.psum_scatter(x, "coef", scatter_dimension=0, tiled=True)
    share = x.shape[0] // count
    me = lax.axis_index("coef")
    total = lax.dynamic_slice_in_dim(x, me * share, share, 0)
    parts = [
        xor_permute(lax.dynamic_slice_in_dim(x, (me ^ d) * share, share, 0), d, ends_only)
        for d in range(count - 1, 0, -1)
    ]
    for part in parts:
        total = total + part
    return total


def gather_rows(x, ends_only=False):
    count = lax.axis_size("coef")
    if not few("coef"):
        return lax.all_gather(x, "coef", axis=0, tiled=True)
    me = lax.axis_index("coef")
    pieces = jnp.stack([x] + [xor_permute(x, d, ends_only) for d in range(1, count)])
    return jnp.concatenate(
        [lax.dynamic_index_in_dim(pieces, me ^ j, 0, keepdims=False) for j in range(count)]
    )


def end_sum(x, distance=1):
    count = lax.axis_size("coef")
    if not few("coef"):
        return lax.psum(x, "coef")
    while distance < count:
        x = x + xor_permute(x, distance, True)
        distance *= 2
    return x


def ends(x):
    count = lax.axis_size("ka")
    if count != 4:
        both = lax.all_gather(x, "ka", axis=0)
        return both[0], both[count - 1]
    me = lax.axis_index("ka")
    across = lax.ppermute(x, "ka", [(0, 2), (3, 1)])
    own = jnp.where((me == 0) | (me == 3), x, across)
    other = lax.ppermute(own, "ka", [(0, 1), (1, 0), (2, 3), (3, 2)])
    even = (me == 0) | (me == 2)
    return jnp.where(even, own, other), jnp.where(even, other, own)


def copy_rows_kernel(pieces, wave, *refs):
    outs = refs[: len(pieces)]
    bufs = refs[len(pieces) : 2 * len(pieces)]
    in_sem, out_sem = refs[2 * len(pieces) :]
    ins = [
        pltpu.make_async_copy(wave.at[pl.ds(low, high - low)], buf, in_sem.at[i])
        for i, ((low, high), buf) in enumerate(zip(pieces, bufs))
    ]
    puts = [pltpu.make_async_copy(buf, out, out_sem.at[i]) for i, (buf, out) in enumerate(zip(bufs, outs))]
    for copy in ins:
        copy.start()
    for get, put in zip(ins, puts):
        get.wait()
        put.start()
    for put in puts:
        put.wait()


def copy_rows(wave, pieces):
    size = wave.shape[1]
    shapes = [(high - low, size) for low, high in pieces]
    return pl.pallas_call(
        functools.partial(copy_rows_kernel, pieces),
        out_shape=[jax.ShapeDtypeStruct(s, F32) for s in shapes],
        in_specs=[HBM],
        out_specs=[HBM] * len(pieces),
        scratch_shapes=[pltpu.VMEM(s, F32) for s in shapes]
        + [pltpu.SemaphoreType.DMA((len(pieces),)), pltpu.SemaphoreType.DMA((len(pieces),))],
        name="copy_rows",
    )(wave)


def cuts(unit, shares):
    bounds = [0]
    for share in shares:
        bounds.append(bounds[-1] + share * unit)
    return list(zip(bounds[:-1], bounds[1:]))


def meet_kernel(flag, at_ref, left_ref, right_ref, total_ref, *refs):
    out_ref = refs[-1]

    @pl.when(pl.program_id(0) == 0)
    def _():
        out_ref[...] = total_ref[...]

    @pl.when(at_ref[flag] == 1)
    def _():
        left, right = split(left_ref[...]), split(right_ref[...])
        dims = (((0,), (0,)), ((), ()))
        size = right_ref.shape[1]
        both = lax.dot_general(left[0], jnp.concatenate(right, axis=1), dims, preferred_element_type=F32)
        rest = lax.dot_general(left[1], right[0], dims, preferred_element_type=F32)
        out_ref[...] += both[:, :size] + (both[:, size:] + rest)


def meet(left, left_at, right, right_at, rows, total, at, flag, behind=()):
    lanes, size = left.shape[1], right.shape[1]
    block = math.gcd(rows, left_at, right_at)
    while block > 1024:
        block //= 2 if block % 2 == 0 else 3
    left_at, right_at = left_at // block, right_at // block

    def left_map(i, at):
        return ((left_at + i) * at[flag], 0)

    def right_map(i, at):
        further = at[0] // block if flag == 3 else 0
        return ((right_at + further + i) * at[flag], 0)

    whole = pl.BlockSpec(total.shape, lambda i, at: (0, 0))
    return pl.pallas_call(
        functools.partial(meet_kernel, flag),
        out_shape=jax.ShapeDtypeStruct(total.shape, F32),
        grid_spec=pltpu.PrefetchScalarGridSpec(
            num_scalar_prefetch=1,
            grid=(rows // block,),
            in_specs=[
                pl.BlockSpec((block, lanes), left_map),
                pl.BlockSpec((block, size), right_map),
                whole,
            ]
            + [ANY] * len(behind),
            out_specs=whole,
        ),
        cost_estimate=pl.CostEstimate(
            flops=6 * rows * lanes * size, bytes_accessed=4 * rows * (lanes + size), transcendentals=0
        ),
        name="meet",
    )(at, left, right, total, *behind)


def cut_kernel(pieces, start, wave, *refs):
    outs = refs[: len(pieces)]
    buf, in_sem, out_sem = refs[len(pieces) :]
    half, _ = buf.shape
    begin = pl.multiple_of(start[0], 8)
    share = half // in_sem.shape[0]
    gets = [
        pltpu.make_async_copy(
            wave.at[pl.ds(begin + i * share, share)], buf.at[pl.ds(i * share, share)], in_sem.at[i]
        )
        for i in range(in_sem.shape[0])
    ]
    puts = [
        pltpu.make_async_copy(
            buf.at[pl.ds(low, high - low), pl.ds(left, right - left)], out, out_sem.at[i]
        )
        for i, (((low, high), (left, right)), out) in enumerate(zip(pieces, outs))
    ]
    for get in gets:
        get.start()
    landed = 0
    for ((low, high), _), put in zip(pieces, puts):
        while landed * share < high:
            gets[landed].wait()
            landed += 1
        put.start()
    for get in gets[landed:]:
        get.wait()
    for put in puts:
        put.wait()


def cut_call(wave, start, half, pieces):
    shapes = [(high - low, right - left) for (low, high), (left, right) in pieces]
    return pl.pallas_call(
        functools.partial(cut_kernel, pieces),
        out_shape=[jax.ShapeDtypeStruct(s, F32) for s in shapes],
        in_specs=[pl.BlockSpec(memory_space=pltpu.SMEM), HBM],
        out_specs=[HBM] * len(shapes),
        scratch_shapes=[
            pltpu.VMEM((half, wave.shape[1]), F32),
            pltpu.SemaphoreType.DMA((6,)),
            pltpu.SemaphoreType.DMA((len(shapes),)),
        ],
        name="cut",
    )(jnp.reshape(start, (1,)).astype(jnp.int32), wave)


FIRSTS = (3, 5, 3, 1)
WIDES = (6, 6)
LATES = (6, 4, 2)


def whole_step(wavefunctions):
    wave = wavefunctions[0]
    count, size = wave.shape
    points = lax.axis_size("ka")
    position = lax.axis_index("ka")
    coefs = lax.axis_size("coef")
    total = count * coefs
    half = count // 2
    unit = half // 12
    wide = size - 128
    forward = [(k, k + 1) for k in range(points - 1)]
    backward = [(k + 1, k) for k in range(points - 1)]
    closing = [(0, points - 1), (points - 1, 0)]
    streamed = []
    start = jnp.where(position == 0, 0, half)
    at_end = (position == 0) | (position == points - 1)
    at = jnp.stack([half - start, position > 0, position < points - 1, at_end]).astype(jnp.int32)

    def stream(*pieces):
        streamed.append(tuple(lax.ppermute(x, "ka", way) for x, way in pieces))

    firsts = cuts(unit, FIRSTS)
    for low, high in firsts:
        up, down = copy_rows(wave, [(low, high), (half + low, half + high)])
        stream((up, forward), (down, backward))

    wides, lates = cuts(unit, WIDES), cuts(unit, LATES)
    blocks = [(rows, (0, wide)) for rows in wides] + [(rows, (wide, size)) for rows in lates]
    up, down = streamed[-2]
    token = lax.ppermute(up[:8, :128] + down[:8, :128], "ka", [(k, k ^ 1) for k in range(points)])
    blocks = cut_call(wave, start, half, blocks)
    for block in blocks:
        stream((block, closing))

    def close(i, rows, block, *behind):
        low, high = rows
        return meet(streamed[i][0], 0, wave, low, high - low, block, at, 3, behind)

    at_later = at_earlier = jnp.zeros((size, size), F32)
    for i, (low, high) in enumerate(firsts):
        up, down = streamed[i]
        at_later = meet(up, 0, wave, low, high - low, at_later, at, 1)
        at_earlier = meet(wave, half + low, down, 0, high - low, at_earlier, at, 2)

    both = jnp.stack([at_later, at_earlier])
    share = size // coefs
    both = scatter_sum(both.reshape(2, coefs, share, size).transpose(1, 0, 2, 3).reshape(2 * size, size))
    margin_share = both[:share] + lax.ppermute(both[share:], "ka", forward)
    early = jnp.zeros((wide, size), F32)
    first = len(firsts)
    early = close(first, wides[0], early, token)
    early = close(first + 1, wides[1], early)
    unitary = polar_call(gather_rows(margin_share), total, early)

    mine = lax.axis_index("coef")
    share = size // coefs
    own = jnp.where(position == 0, jnp.eye(size, dtype=F32), unitary)
    product = lax.dynamic_slice_in_dim(own, mine * share, share, 0)
    for k in range(1, points - 1):
        came = lax.ppermute(product, "ka", [(k, k + 1)])
        longer = lax.dot_general(came, own, (((1,), (0,)), ((), ())), precision=lax.Precision.HIGH)
        product = jnp.where(position == k + 1, longer, product)
    later = gather_rows(product)

    pair = early + xor_permute(early, 1, True) if few("coef") else early
    late = close(first + 2, lates[0], jnp.zeros((128, size), F32), product, pair)
    early = ends(end_sum(pair, 2) if few("coef") else end_sum(early))
    late = close(first + 3, lates[1], late, *early)
    late = close(first + 4, lates[2], late)
    late = ends(end_sum(late))
    rows, turned = [jnp.concatenate(pair) for pair in zip(early, late)]
    return rotate_call(rows, turned, later, wave, total)[None]


def solution(mesh):
    spec = P(("strings", "ka"), "coef", None)
    return jax.shard_map(whole_step, mesh=mesh, in_specs=(spec,), out_specs=spec, check_vma=False)
```

```python
import functools
import math

import jax
import jax.numpy as jnp
from jax import lax
from jax.experimental import pallas as pl
from jax.experimental.pallas import tpu as pltpu
from jax.sharding import PartitionSpec as P


NS_ITERS = 3
F32 = jnp.float32
BF16 = jnp.bfloat16


def split(x):
    high = x.astype(BF16)
    return high, (x - high.astype(F32)).astype(BF16)


def dot(a, b):
    return lax.dot_general(a, b, (((1,), (0,)), ((), ())), preferred_element_type=F32)


def product3(a, b):
    size = b[0].shape[1]
    wide = dot(a[0], jnp.concatenate(b, axis=1))
    return wide[:, :size] + (wide[:, size:] + dot(a[1], b[0]))


def polar(matrix, total):
    size = matrix.shape[0]
    margin = matrix * (1.0 / total)
    scale = jnp.sqrt(size * (jnp.sum(margin * margin) / (size * size)) + 1e-06)
    iterate = margin / scale
    for _ in range(NS_ITERS):
        parts = split(iterate)
        gram = product3(split(iterate.T), parts)
        iterate = 1.5 * iterate - 0.5 * product3(parts, split(gram))
    return iterate


def polar_kernel(total, sum_ref, *refs):
    refs[-1][...] = polar(sum_ref[...], total)


VMEM = pl.BlockSpec(memory_space=pltpu.VMEM)
HBM = pl.BlockSpec(memory_space=pltpu.HBM)
ANY = pl.BlockSpec(memory_space=pl.ANY)


def polar_call(matrix, total, behind):
    return pl.pallas_call(
        functools.partial(polar_kernel, total),
        out_shape=jax.ShapeDtypeStruct(matrix.shape, F32),
        in_specs=[VMEM, ANY],
        out_specs=VMEM,
        name="polar",
    )(matrix, behind)


def rotate_kernel(total, rows_ref, turned_ref, later_ref, wave, out, wave_buf, out_buf, near_ref, rest_ref, low_ref, in_sem, out_sem):
    size = wave_buf.shape[1]
    block = out_buf.shape[1]
    steps = wave_buf.shape[0] // block
    main = size // 256 * 256
    rest = size - main

    def fetch(c):
        piece = pl.ds(pl.multiple_of(c * block, block), block)
        return pltpu.make_async_copy(wave.at[piece], wave_buf.at[piece], in_sem.at[c])

    def put(c):
        piece = pl.ds(pl.multiple_of(c * block, block), block)
        return pltpu.make_async_copy(out_buf.at[c % 2], out.at[piece], out_sem.at[c % 2])

    for c in range(steps):
        fetch(c).start()
    closing = polar(rows_ref[...] + turned_ref[...].T, total)
    high, low = split(product3(split(later_ref[...].T), split(closing.T)))
    near_ref[0:size] = high[:, :main]
    near_ref[size:] = high[:, :main]
    rest_ref[0:size, :rest] = high[:, main:]
    rest_ref[size:, :rest] = high[:, main:]
    rest_ref[0:size, rest:] = low[:, main:]
    rest_ref[size:, rest:] = jnp.zeros((size, rest), BF16)
    low_ref[...] = low[:, :main]

    def body(c, _):
        fetch(c).wait()

        @pl.when(c >= 2)
        def _():
            put(c - 2).wait()

        high, low = split(wave_buf[pl.ds(pl.multiple_of(c * block, block), block)])
        both = jnp.concatenate([high, low], axis=1)
        out_buf[c % 2, :, :main] = dot(both, near_ref[...]) + dot(high, low_ref[...])
        wide = dot(both, rest_ref[...])
        out_buf[c % 2, :, main:] = wide[:, :rest] + wide[:, rest:]
        put(c).start()
        return 0

    lax.fori_loop(0, steps, body, 0)
    for c in range(max(steps - 2, 0), steps):
        put(c).wait()


def rotate_call(rows, turned, later, wave, total):
    count, size = wave.shape
    block = 1024
    while count % block:
        block //= 2
    main = size // 256 * 256
    rest = size - main
    hbm = pl.BlockSpec(memory_space=pltpu.HBM)
    return pl.pallas_call(
        functools.partial(rotate_kernel, total),
        out_shape=jax.ShapeDtypeStruct(wave.shape, F32),
        in_specs=[VMEM, VMEM, VMEM, hbm],
        out_specs=hbm,
        scratch_shapes=[
            pltpu.VMEM((count, size), F32),
            pltpu.VMEM((2, block, size), F32),
            pltpu.VMEM((2 * size, main), BF16),
            pltpu.VMEM((2 * size, 2 * rest), BF16),
            pltpu.VMEM((size, main), BF16),
            pltpu.SemaphoreType.DMA((count // block,)),
            pltpu.SemaphoreType.DMA((2,)),
        ],
        name="rotate",
    )(rows, turned, later, wave)


def few(axis, mesh=None):
    return (mesh.shape[axis] if mesh else lax.axis_size(axis)) in (2, 4)


def xor_permute(x, distance, ends_only=False):
    points, count = lax.axis_size("ka"), lax.axis_size("coef")
    some = (0, points - 1) if ends_only else range(points)
    route = [(k * count + i, k * count + (i ^ distance)) for k in some for i in range(count)]
    return lax.ppermute(x, ("ka", "coef"), route)


def scatter_sum(x, ends_only=False):
    count = lax.axis_size("coef")
    if not few("coef"):
        return lax.psum_scatter(x, "coef", scatter_dimension=0, tiled=True)
    share = x.shape[0] // count
    me = lax.axis_index("coef")
    total = lax.dynamic_slice_in_dim(x, me * share, share, 0)
    parts = [
        xor_permute(lax.dynamic_slice_in_dim(x, (me ^ d) * share, share, 0), d, ends_only)
        for d in range(count - 1, 0, -1)
    ]
    for part in parts:
        total = total + part
    return total


def gather_rows(x, ends_only=False):
    count = lax.axis_size("coef")
    if not few("coef"):
        return lax.all_gather(x, "coef", axis=0, tiled=True)
    me = lax.axis_index("coef")
    pieces = jnp.stack([x] + [xor_permute(x, d, ends_only) for d in range(1, count)])
    return jnp.concatenate(
        [lax.dynamic_index_in_dim(pieces, me ^ j, 0, keepdims=False) for j in range(count)]
    )


def end_sum(x):
    count = lax.axis_size("coef")
    if not few("coef"):
        return lax.psum(x, "coef")
    distance = 1
    while distance < count:
        x = x + xor_permute(x, distance, True)
        distance *= 2
    return x


def ends(x):
    count = lax.axis_size("ka")
    if count != 4:
        both = lax.all_gather(x, "ka", axis=0)
        return both[0], both[count - 1]
    me = lax.axis_index("ka")
    across = lax.ppermute(x, "ka", [(0, 2), (3, 1)])
    own = jnp.where((me == 0) | (me == 3), x, across)
    other = lax.ppermute(own, "ka", [(0, 1), (1, 0), (2, 3), (3, 2)])
    even = (me == 0) | (me == 2)
    return jnp.where(even, own, other), jnp.where(even, other, own)


def copy_rows_kernel(pieces, wave, *refs):
    outs = refs[: len(pieces)]
    bufs = refs[len(pieces) : 2 * len(pieces)]
    in_sem, out_sem = refs[2 * len(pieces) :]
    ins = [
        pltpu.make_async_copy(wave.at[pl.ds(low, high - low)], buf, in_sem.at[i])
        for i, ((low, high), buf) in enumerate(zip(pieces, bufs))
    ]
    puts = [pltpu.make_async_copy(buf, out, out_sem.at[i]) for i, (buf, out) in enumerate(zip(bufs, outs))]
    for copy in ins:
        copy.start()
    for get, put in zip(ins, puts):
        get.wait()
        put.start()
    for put in puts:
        put.wait()


def copy_rows(wave, pieces):
    size = wave.shape[1]
    shapes = [(high - low, size) for low, high in pieces]
    return pl.pallas_call(
        functools.partial(copy_rows_kernel, pieces),
        out_shape=[jax.ShapeDtypeStruct(s, F32) for s in shapes],
        in_specs=[HBM],
        out_specs=[HBM] * len(pieces),
        scratch_shapes=[pltpu.VMEM(s, F32) for s in shapes]
        + [pltpu.SemaphoreType.DMA((len(pieces),)), pltpu.SemaphoreType.DMA((len(pieces),))],
        name="copy_rows",
    )(wave)


def cuts(unit, shares):
    bounds = [0]
    for share in shares:
        bounds.append(bounds[-1] + share * unit)
    return list(zip(bounds[:-1], bounds[1:]))


def meet_kernel(flag, at_ref, left_ref, right_ref, total_ref, *refs):
    out_ref = refs[-1]

    @pl.when(pl.program_id(0) == 0)
    def _():
        out_ref[...] = total_ref[...]

    @pl.when(at_ref[flag] == 1)
    def _():
        left, right = split(left_ref[...]), split(right_ref[...])
        dims = (((0,), (0,)), ((), ()))
        size = right_ref.shape[1]
        both = lax.dot_general(left[0], jnp.concatenate(right, axis=1), dims, preferred_element_type=F32)
        rest = lax.dot_general(left[1], right[0], dims, preferred_element_type=F32)
        out_ref[...] += both[:, :size] + (both[:, size:] + rest)


def meet(left, left_at, right, right_at, rows, total, at, flag, behind=()):
    lanes, size = left.shape[1], right.shape[1]
    block = math.gcd(rows, left_at, right_at)
    while block > 1024:
        block //= 2 if block % 2 == 0 else 3
    left_at, right_at = left_at // block, right_at // block

    def left_map(i, at):
        return ((left_at + i) * at[flag], 0)

    def right_map(i, at):
        further = at[0] // block if flag == 3 else 0
        return ((right_at + further + i) * at[flag], 0)

    whole = pl.BlockSpec(total.shape, lambda i, at: (0, 0))
    return pl.pallas_call(
        functools.partial(meet_kernel, flag),
        out_shape=jax.ShapeDtypeStruct(total.shape, F32),
        grid_spec=pltpu.PrefetchScalarGridSpec(
            num_scalar_prefetch=1,
            grid=(rows // block,),
            in_specs=[
                pl.BlockSpec((block, lanes), left_map),
                pl.BlockSpec((block, size), right_map),
                whole,
            ]
            + [ANY] * len(behind),
            out_specs=whole,
        ),
        cost_estimate=pl.CostEstimate(
            flops=6 * rows * lanes * size, bytes_accessed=4 * rows * (lanes + size), transcendentals=0
        ),
        name="meet",
    )(at, left, right, total, *behind)


def cut_kernel(pieces, start, wave, *refs):
    outs = refs[: len(pieces)]
    buf, in_sem, out_sem = refs[len(pieces) :]
    half, _ = buf.shape
    begin = pl.multiple_of(start[0], 8)
    share = half // in_sem.shape[0]
    gets = [
        pltpu.make_async_copy(
            wave.at[pl.ds(begin + i * share, share)], buf.at[pl.ds(i * share, share)], in_sem.at[i]
        )
        for i in range(in_sem.shape[0])
    ]
    puts = [
        pltpu.make_async_copy(
            buf.at[pl.ds(low, high - low), pl.ds(left, right - left)], out, out_sem.at[i]
        )
        for i, (((low, high), (left, right)), out) in enumerate(zip(pieces, outs))
    ]
    for get in gets:
        get.start()
    landed = 0
    for ((low, high), _), put in zip(pieces, puts):
        while landed * share < high:
            gets[landed].wait()
            landed += 1
        put.start()
    for get in gets[landed:]:
        get.wait()
    for put in puts:
        put.wait()


def cut_call(wave, start, half, pieces):
    shapes = [(high - low, right - left) for (low, high), (left, right) in pieces]
    return pl.pallas_call(
        functools.partial(cut_kernel, pieces),
        out_shape=[jax.ShapeDtypeStruct(s, F32) for s in shapes],
        in_specs=[pl.BlockSpec(memory_space=pltpu.SMEM), HBM],
        out_specs=[HBM] * len(shapes),
        scratch_shapes=[
            pltpu.VMEM((half, wave.shape[1]), F32),
            pltpu.SemaphoreType.DMA((6,)),
            pltpu.SemaphoreType.DMA((len(shapes),)),
        ],
        name="cut",
    )(jnp.reshape(start, (1,)).astype(jnp.int32), wave)


FIRSTS = (3, 5, 3, 1)
WIDES = (6, 6)
LATES = (6, 5, 1)


def whole_step(wavefunctions):
    wave = wavefunctions[0]
    count, size = wave.shape
    points = lax.axis_size("ka")
    position = lax.axis_index("ka")
    coefs = lax.axis_size("coef")
    total = count * coefs
    half = count // 2
    unit = half // 12
    wide = size - 128
    forward = [(k, k + 1) for k in range(points - 1)]
    backward = [(k + 1, k) for k in range(points - 1)]
    closing = [(0, points - 1), (points - 1, 0)]
    streamed = []
    start = jnp.where(position == 0, 0, half)
    at_end = (position == 0) | (position == points - 1)
    at = jnp.stack([half - start, position > 0, position < points - 1, at_end]).astype(jnp.int32)

    def stream(*pieces):
        streamed.append(tuple(lax.ppermute(x, "ka", way) for x, way in pieces))

    firsts = cuts(unit, FIRSTS)
    for low, high in firsts:
        up, down = copy_rows(wave, [(low, high), (half + low, half + high)])
        stream((up, forward), (down, backward))

    wides, lates = cuts(unit, WIDES), cuts(unit, LATES)
    blocks = [(rows, (0, wide)) for rows in wides] + [(rows, (wide, size)) for rows in lates]
    up, down = streamed[-2]
    token = lax.ppermute(up[:8, :128] + down[:8, :128], "ka", [(k, k ^ 1) for k in range(points)])
    blocks = cut_call(wave, start, half, blocks)
    for block in blocks:
        stream((block, closing))

    def close(i, rows, block, *behind):
        low, high = rows
        return meet(streamed[i][0], 0, wave, low, high - low, block, at, 3, behind)

    at_later = at_earlier = jnp.zeros((size, size), F32)
    for i, (low, high) in enumerate(firsts):
        up, down = streamed[i]
        at_later = meet(up, 0, wave, low, high - low, at_later, at, 1)
        at_earlier = meet(wave, half + low, down, 0, high - low, at_earlier, at, 2)

    both = jnp.stack([at_later, at_earlier])
    share = size // coefs
    both = scatter_sum(both.reshape(2, coefs, share, size).transpose(1, 0, 2, 3).reshape(2 * size, size))
    margin_share = both[:share] + lax.ppermute(both[share:], "ka", forward)
    early = jnp.zeros((wide, size), F32)
    first = len(firsts)
    early = close(first, wides[0], early, token)
    early = close(first + 1, wides[1], early)
    margin = gather_rows(margin_share)
    unitary = polar_call(margin, total, early)

    mine = lax.axis_index("coef")
    share = size // coefs
    own = jnp.where(position == 0, jnp.eye(size, dtype=F32), unitary)
    product = lax.dynamic_slice_in_dim(own, mine * share, share, 0)
    for k in range(1, points - 1):
        came = lax.ppermute(product, "ka", [(k, k + 1)])
        longer = lax.dot_general(came, own, (((1,), (0,)), ((), ())), precision=lax.Precision.HIGH)
        product = jnp.where(position == k + 1, longer, product)
    later = gather_rows(product)

    early = ends(end_sum(early))
    late = close(first + 2, lates[0], jnp.zeros((128, size), F32))
    late = close(first + 3, lates[1], late)
    late = close(first + 4, lates[2], late)
    late = ends(end_sum(late))
    rows, turned = [jnp.concatenate(pair) for pair in zip(early, late)]
    return rotate_call(rows, turned, later, wave, total)[None]


def solution(mesh):
    spec = P(("strings", "ka"), "coef", None)
    return jax.shard_map(whole_step, mesh=mesh, in_specs=(spec,), out_specs=spec, check_vma=False)
```
